32 devices in a mesh: vec: 16 (over z, y, x), row: 2 (over core).
Axes of the slice: x: 2, y: 2, z: 4, core: 2. Of those that a mesh axis runs over, the one named last changes fastest.
Arguments:
- vectors: bfloat16 [2, 4096, 1024], P('row', 'vec'), may hold values from -6 to 6
- rotation: bfloat16 [1024, 1024], P(None, 'vec'), may hold values from -0.1875 to 0.1875
- blocks: bfloat16 [64, 8, 128, 128], P('row'), may hold values from -0.125 to 0.125
- column_blocks: int32 [64, 8], P('row'), may hold values from -2 to 65, as said below
Outputs:
- filtered: bfloat16 [2, 4096, 1024], P('row', 'vec')
The draws below stay inside these ranges and needn't reach their ends.
Inputs may be any that keep to these rules, and one draw needn't show every extreme that they name: `column_blocks`: block row r of partition p = r // 32 lists 8 distinct column blocks between p * 32 - 2 and p * 32 + 33; the first block row of every partition lists the lowest of these and the last one the highest; column blocks outside 0 to 63 stand for zeros.
All inputs are finite; a program needn't handle non-finite values.
Results may differ from the reference program's by a relative error of at most 0.006.
Values may be sent and summed in bfloat16 or wider, within the bound.
No kernel may reach another device: no remote copies, remote signals or barrier semaphores. Data moves between devices by JAX's collectives and lax.ppermute only.
A program may use at most 64 MiB of HBM per device.

```python
import jax
import jax.numpy as jnp

K = 1024
BS = 128
NNZB = 8
HB = 2
STEPS = 4
RB = 32
NBLK = 64
ROWS_PART = 4096
NPART = 2


def draw_column_blocks(key, part):
    candidates = RB + 2 * HB
    subkeys = jax.random.split(key, NBLK)
    shuffled = jax.vmap(lambda sub: jax.random.permutation(sub, candidates))(subkeys)
    chosen = shuffled[:, :NNZB].astype(jnp.int32)
    within = jnp.arange(NBLK, dtype=jnp.int32) % RB
    required = jnp.where(within == 0, 0, jnp.where(within == RB - 1, candidates - 1, -1)).astype(jnp.int32)
    present = jnp.any(chosen == required[:, None], axis=1)
    replaced = jnp.where((required >= 0) & jnp.logical_not(present), required, chosen[:, NNZB - 1])
    chosen = chosen.at[:, NNZB - 1].set(replaced)
    first_block = jnp.arange(NBLK, dtype=jnp.int32) // RB * RB - HB
    return (chosen + first_block[:, None]).astype(jnp.int32)


def levels(own_key, shape, pieces, low, high):
    loudness = 1.0
    for position, shards_of in pieces:
        heights = jax.random.uniform(jax.random.fold_in(jax.random.fold_in(own_key, 6), position), (shards_of,), jnp.float32, low / len(pieces), high / len(pieces))
        loudness = loudness * jnp.repeat(jnp.exp(heights), shape[position] // shards_of).reshape((-1,) + (1,) * (len(shape) - 1 - position))
    return loudness


def bell_draw(rng, shape, spread, bound, cuts=(), kind=jnp.bfloat16):
    loudness = levels(rng, shape, cuts, -0.22, 0.18) if cuts else 1.0
    result = jax.random.normal(rng, shape, jnp.float32) * spread * loudness
    return jnp.minimum(jnp.maximum(result, -bound), bound).astype(kind)


def setup_inputs(seed: int = 0) -> dict:
    key_of = jax.random.split(jax.random.key(seed), 5)
    vectors = bell_draw(key_of[0], (NPART, ROWS_PART, K), 1.0, 6.0, ((0, 2), (1, 16)))
    rotation = bell_draw(key_of[1], (K, K), K ** -0.5, 0.1875, ((1, 16),))
    blocks = bell_draw(key_of[2], (NBLK, NNZB, BS, BS), (2 * NNZB * BS) ** -0.5, 0.125, ((0, 2),))
    column_blocks = draw_column_blocks(jax.random.fold_in(key_of[4], 71), 0)
    return dict(vectors=vectors, rotation=rotation, blocks=blocks, column_blocks=column_blocks)


centre = 0.3
half_width = 1.2


def apply_matrix(field, blocks, column_blocks):
    padded = jnp.pad(field, ((HB * BS, HB * BS), (0, 0)))
    stacked = padded.reshape(NBLK + 2 * HB, BS, K)
    picked = stacked[column_blocks + HB]
    product = jnp.einsum('rjab,rjbk->rak', blocks.astype(jnp.float32), picked.astype(jnp.float32))
    return product.reshape(NBLK * BS, K)


def reference(vectors, rotation, blocks, column_blocks):
    flattened = vectors.reshape(NBLK * BS, K)
    rotated = jnp.dot(flattened, rotation, preferred_element_type=jnp.float32).astype(jnp.bfloat16)
    previous = rotated.astype(jnp.float32)
    current = (apply_matrix(rotated, blocks, column_blocks) - centre * previous) / half_width
    for turn_index in range(STEPS - 1):
        operand = current.astype(jnp.bfloat16)
        following = 2.0 * (apply_matrix(operand, blocks, column_blocks) - centre * current) / half_width - previous
        previous = current
        current = following
    return current.astype(jnp.bfloat16).reshape(NPART, ROWS_PART, K)
```

```python
import functools

import jax
import jax.numpy as jnp
from jax import lax
from jax.experimental import pallas as pl
from jax.experimental.pallas import tpu as pltpu
from jax.sharding import PartitionSpec as P

HB = 2
STEPS = 4
UNROLL = 4

centre = 0.3
half_width = 1.2

VMEM = pl.BlockSpec(memory_space=pltpu.VMEM)
SMEM = pl.BlockSpec(memory_space=pltpu.SMEM)


def step_kernel(first, last, count, place, offsets, held, low, high, blocks, *refs):
    if first:
        previous = current = held
        outs = refs
    else:
        current, previous = refs[:2]
        outs = refs[2:]
    outs, field = outs[:-1], outs[-1]
    rows, listed = blocks.shape[:2]
    field[HB : HB + rows] = held[...]
    if count == 2:
        received = low[...]
        nothing = jnp.zeros_like(received)
        field[:HB] = jnp.where(place[0] == 1, received, nothing)
        field[HB + rows :] = jnp.where(place[0] == 0, received, nothing)
    else:
        field[:HB] = low[...]
        field[HB + rows :] = high[...]
    operand = outs[0]

    def body(row, carry):
        picked = jnp.concatenate([field[offsets[row, j]] for j in range(listed)], axis=1)
        matrix = jnp.concatenate([blocks[row, j] for j in range(listed)], axis=1)
        product = lax.dot_general(
            picked, matrix, (((1,), (1,)), ((), ())), preferred_element_type=jnp.float32
        )
        if first:
            following = (product - centre * current[row].astype(jnp.float32)) / half_width
        else:
            following = (
                2.0 * (product - centre * current[row]) / half_width
                - previous[row].astype(jnp.float32)
            )
        operand[row] = following.astype(jnp.bfloat16)
        if not last:
            outs[1][row] = following
        return carry

    lax.fori_loop(0, rows, body, 0, unroll=UNROLL)
    if not last:
        if count == 2:
            start = jnp.where(place[0] == 0, rows - HB, 0)
            outs[2][...] = operand[pl.ds(start, HB)]
        else:
            outs[2][...] = operand[:HB]
            outs[3][...] = operand[rows - HB :]


def filter_step(turn, count, place, offsets, held, halo, blocks, state):
    first, last = turn == 0, turn == STEPS - 1
    rows, columns, width = held.shape
    edge = jax.ShapeDtypeStruct((HB, columns, width), jnp.bfloat16)
    out_shape = [jax.ShapeDtypeStruct(held.shape, jnp.bfloat16)]
    if not last:
        out_shape.append(jax.ShapeDtypeStruct(held.shape, jnp.float32))
        out_shape += [edge] if count == 2 else [edge, edge]
    flops = 2 * blocks.size * columns
    return pl.pallas_call(
        functools.partial(step_kernel, first, last, count),
        out_shape=out_shape,
        in_specs=[SMEM, SMEM] + [VMEM] * (4 + len(state)),
        out_specs=[VMEM] * len(out_shape),
        scratch_shapes=[pltpu.VMEM((rows + 2 * HB, columns, width), jnp.bfloat16)],
        compiler_params=pltpu.CompilerParams(vmem_limit_bytes=8 * 2**20),
        cost_estimate=pl.CostEstimate(
            flops=flops, bytes_accessed=2 * blocks.size, transcendentals=0
        ),
        name="filter_step",
    )(place, offsets, held, *halo, blocks, *state)


def exchange(count, edges):
    if count == 2:
        received = lax.ppermute(edges[0], "row", [(0, 1), (1, 0)])
        return received, received
    first, last = edges
    forward = [(i, i + 1) for i in range(count - 1)]
    backward = [(i + 1, i) for i in range(count - 1)]
    return lax.ppermute(last, "row", forward), lax.ppermute(first, "row", backward)


def filter_panel(held, blocks, column_blocks):
    count = lax.axis_size("row")
    place = lax.axis_index("row")
    rows = held.shape[0]
    offsets = column_blocks - (place * rows - HB)
    place = place.astype(jnp.int32)[None]
    if count == 2:
        edges = [lax.dynamic_slice_in_dim(held, jnp.where(place[0] == 0, rows - HB, 0), HB)]
    else:
        edges = [held[:HB], held[rows - HB :]]
    operand, state = held, ()
    older, newer = None, held
    for turn in range(STEPS):
        halo = exchange(count, edges)
        outs = filter_step(turn, count, place, offsets, operand, halo, blocks, state)
        operand = outs[0]
        if turn < STEPS - 1:
            edges = outs[2:]
            older, newer = newer, outs[1]
            state = (newer, older)
    return operand


def gather_rotation(shard):
    vec = lax.axis_size("vec")
    side = lax.rem(lax.axis_index("row"), 2)
    half = shard.shape[0] // 2
    held = lax.dynamic_slice_in_dim(shard, side * half, half)[None]
    bits = []
    bit = 1
    while bit < vec:
        bits.append(bit)
        bit *= 2
    for bit in reversed(bits):
        other = lax.ppermute(held, "vec", [(i, i ^ bit) for i in range(vec)])
        held = jnp.concatenate([held[:, None], other[:, None]], axis=1).reshape(
            (-1,) + held.shape[1:]
        )
    other = lax.ppermute(held, "row", [(i, i ^ 1) for i in range(lax.axis_size("row"))])
    return held, other


def rotate_kernel(place, filtered, own, other, out, turned):
    vec, groups, columns, width = filtered.shape
    me, side = place[0], place[1]
    for group in range(groups):
        turned[group * width : (group + 1) * width, :] = filtered[:, group].reshape(
            vec * columns, width
        ).T
    rows = turned[...]
    span = max(1, 256 // columns)
    for start in range(0, vec, span):
        pieces = []
        for index in range(start, start + span):
            slot = me ^ index
            mine, theirs = own[slot], other[slot]
            pieces.append(jnp.where(side == 0, mine, theirs))
            pieces.append(jnp.where(side == 0, theirs, mine))
        matrix = jnp.concatenate(pieces, axis=0)
        product = lax.dot_general(
            rows, matrix, (((1,), (1,)), ((), ())), preferred_element_type=jnp.float32
        )
        out[:, start * columns : (start + span) * columns] = product.astype(jnp.bfloat16)


def rotate(filtered, own, other):
    vec, groups, columns, width = filtered.shape
    place = jnp.stack([lax.axis_index("vec"), lax.rem(lax.axis_index("row"), 2)]).astype(jnp.int32)
    return pl.pallas_call(
        rotate_kernel,
        out_shape=jax.ShapeDtypeStruct((groups * width, vec * columns), jnp.bfloat16),
        in_specs=[SMEM, VMEM, VMEM, VMEM],
        out_specs=VMEM,
        scratch_shapes=[pltpu.VMEM((groups * width, vec * columns), jnp.bfloat16)],
        compiler_params=pltpu.CompilerParams(vmem_limit_bytes=16 * 2**20),
        name="rotate",
    )(place, filtered, own, other)


def local(vectors, rotation, blocks, column_blocks):
    vec = lax.axis_size("vec")
    own_rows = vectors[0]
    rows, total = own_rows.shape
    columns = total // vec
    width = blocks.shape[-1]
    lanes = min(rows, width)
    groups = rows // lanes
    part = width // lanes
    sent = jnp.transpose(own_rows.reshape(groups, lanes, vec, columns), (2, 0, 3, 1))
    got = lax.all_to_all(sent, "vec", split_axis=0, concat_axis=0, tiled=True)
    own, other = gather_rotation(jnp.transpose(rotation))
    held = got.reshape(-1, part, columns, lanes).swapaxes(1, 2).reshape(-1, columns, width)
    filtered = filter_panel(held, blocks, column_blocks)
    back = filtered.reshape(-1, columns, part, lanes).swapaxes(1, 2)
    back = back.reshape(vec, groups, columns, lanes)
    returned = lax.all_to_all(back, "vec", split_axis=0, concat_axis=0, tiled=True)
    return rotate(returned, own, other)[None]


def solution(mesh):
    placed = (P("row", "vec", None), P(None, "vec"), P("row", None, None, None), P("row", None))
    return jax.shard_map(
        local, mesh=mesh, in_specs=placed, out_specs=P("row", "vec", None), check_vma=False
    )
```

```python
import functools

import jax
import jax.numpy as jnp
from jax import lax
from jax.experimental import pallas as pl
from jax.experimental.pallas import tpu as pltpu
from jax.sharding import PartitionSpec as P


HB = 2
STEPS = 4
UNROLL = 8
TURNED = 4
DIRECT = 2

centre = 0.3
half_width = 1.2

VMEM = pl.BlockSpec(memory_space=pltpu.VMEM)
SMEM = pl.BlockSpec(memory_space=pltpu.SMEM)
ANY = pl.BlockSpec(memory_space=pl.ANY)


def in_hbm(array):
    return pltpu.with_memory_space_constraint(array, pltpu.HBM)


def identity(size):
    rows = lax.broadcasted_iota(jnp.int32, (size, size), 0)
    columns = lax.broadcasted_iota(jnp.int32, (size, size), 1)
    return (rows == columns).astype(jnp.bfloat16)


def turned_by(unit, block):
    return lax.dot_general(
        unit, block, (((1,), (1,)), ((), ())), preferred_element_type=jnp.float32
    ).astype(jnp.bfloat16)


def prepare_kernel(place, vectors, shard, sent, half, landing, leaving, arrived):
    groups, vec, columns, lanes = leaving.shape
    rows = half.shape[1]
    fetch = [
        pltpu.make_async_copy(
            vectors.at[0, pl.ds(group * lanes, lanes)], landing.at[group], arrived.at[group]
        )
        for group in range(groups)
    ]
    pick = pltpu.make_async_copy(
        shard.at[pl.ds(pl.multiple_of(place[1] * rows, rows), rows)],
        half.at[0],
        arrived.at[groups],
    )
    for copy in fetch:
        copy.start()
    pick.start()
    span = max(1, 256 // columns)
    unit = identity(span * columns)
    for group in range(groups):
        fetch[group].wait()
        for start in range(0, vec, span):
            piece = landing[group, :, start * columns : (start + span) * columns]
            leaving[group, start : start + span] = turned_by(unit, piece).reshape(
                span, columns, lanes
            )
        fetch[group] = pltpu.make_async_copy(
            leaving.at[group], sent.at[:, group], arrived.at[group]
        )
        fetch[group].start()
    pick.wait()
    for copy in fetch:
        copy.wait()


def prepare(place, vectors, shard, groups, lanes):
    columns, total = shard.shape
    return pl.pallas_call(
        prepare_kernel,
        out_shape=(
            pltpu.HBM((total // columns, groups, columns, lanes), jnp.bfloat16),
            jax.ShapeDtypeStruct((1, columns // 2, total), jnp.bfloat16),
        ),
        in_specs=[SMEM, ANY, ANY],
        out_specs=(ANY, VMEM),
        scratch_shapes=[
            pltpu.VMEM((groups, lanes, total), jnp.bfloat16),
            pltpu.VMEM((groups, total // columns, columns, lanes), jnp.bfloat16),
            pltpu.SemaphoreType.DMA((groups + 1,)),
        ],
        compiler_params=pltpu.CompilerParams(vmem_limit_bytes=8 * 2**20),
        name="prepare",
    )(place, in_hbm(vectors), in_hbm(shard))


def turn_kernel(blocks, turned):
    rows, listed, width = blocks.shape[:3]
    unit = identity(2 * width)
    for row in range(rows):
        for j in range(0, listed, 2):
            pair = jnp.concatenate([blocks[row, j], blocks[row, j + 1]], axis=1)
            turned[row, j * width : (j + 2) * width, :] = turned_by(unit, pair)


def turn_blocks(blocks, first, rows):
    listed, width = blocks.shape[1:3]
    skipped = first // TURNED
    size = rows * listed * width * width
    return pl.pallas_call(
        turn_kernel,
        grid=(rows // TURNED,),
        out_shape=pltpu.HBM((rows, listed * width, width), jnp.bfloat16),
        in_specs=[
            pl.BlockSpec((TURNED, listed, width, width), lambda row: (row + skipped, 0, 0, 0))
        ],
        out_specs=pl.BlockSpec((TURNED, listed * width, width), lambda row: (row, 0, 0)),
        compiler_params=pltpu.CompilerParams(vmem_limit_bytes=16 * 2**20),
        cost_estimate=pl.CostEstimate(
            flops=4 * width * size, bytes_accessed=4 * size, transcendentals=0
        ),
        name="turn_blocks",
    )(in_hbm(blocks))


def load_kernel(source, out, arrived):
    copy = pltpu.make_async_copy(source, out, arrived)
    copy.start()
    copy.wait()


def load_head(head):
    return pl.pallas_call(
        load_kernel,
        out_shape=jax.ShapeDtypeStruct(head.shape, head.dtype),
        in_specs=[ANY],
        out_specs=VMEM,
        scratch_shapes=[pltpu.SemaphoreType.DMA],
        compiler_params=pltpu.CompilerParams(vmem_limit_bytes=4 * 2**20),
        cost_estimate=pl.CostEstimate(
            flops=0, bytes_accessed=2 * head.size, transcendentals=0
        ),
        name="load_head",
    )(in_hbm(head))


def step_kernel(first, last, count, place, listing, held, low, high, head, tail, *refs):
    refs = list(refs)
    moved = refs.pop()
    field = refs.pop()
    if first:
        source, tail = tail, refs.pop()

        def load(chunk):
            return pltpu.make_async_copy(
                source.at[pl.ds(chunk * UNROLL, UNROLL)],
                tail.at[pl.ds(chunk * UNROLL, UNROLL)],
                moved.at[chunk],
            )

        for chunk in range(tail.shape[0] // UNROLL):
            load(chunk).start()
        previous = current = held
    else:
        current, previous = refs[:2]
        refs = refs[2:]
    if last:
        result, operand = refs

        def store(chunk):
            some = pl.ds(chunk * UNROLL, UNROLL)
            return pltpu.make_async_copy(operand.at[some], result.at[some], moved.at[chunk])

    else:
        operand = refs[0]
    listed, rows = listing.shape
    shift = place[0] * rows - HB
    field[HB : HB + rows] = held[...]
    if count == 2:
        received = low[...]
        nothing = jnp.zeros_like(received)
        field[:HB] = jnp.where(place[0] == 1, received, nothing)
        field[HB + rows :] = jnp.where(place[0] == 0, received, nothing)
    else:
        field[:HB] = low[...]
        field[HB + rows :] = high[...]

    def one(row, matrix):
        picked = jnp.concatenate(
            [field[listing[j, row] - shift] for j in range(listed)], axis=1
        )
        product = jnp.dot(picked, matrix, preferred_element_type=jnp.float32)
        if first:
            following = (product - centre * current[row].astype(jnp.float32)) / half_width
        else:
            following = (
                2.0 * (product - centre * current[row]) / half_width
                - previous[row].astype(jnp.float32)
            )
        operand[row] = following.astype(jnp.bfloat16)
        if not last:
            refs[1][row] = following

    for row in range(UNROLL):
        one(row, head[row])
    if last:
        store(0).start()

    def body(chunk, carry):
        if first:
            load(chunk - 1).wait()
        for index in range(UNROLL):
            one(chunk * UNROLL + index, tail[(chunk - 1) * UNROLL + index])
        if last:
            store(chunk).start()
        return carry

    lax.fori_loop(1, rows // UNROLL, body, 0)
    if last:
        for chunk in range(rows // UNROLL):
            store(chunk).wait()
    elif count == 2:
        start = jnp.where(place[0] == 0, rows - HB, 0)
        refs[2][...] = operand[pl.ds(start, HB)]
    else:
        refs[2][...] = operand[:HB]
        refs[3][...] = operand[rows - HB :]


def filter_step(turn, count, place, listing, held, halo, head, tail, state):
    first, last = turn == 0, turn == STEPS - 1
    rows, columns, width = held.shape
    edge = jax.ShapeDtypeStruct((HB, columns, width), jnp.bfloat16)
    args = [place, listing, held, *halo, head, in_hbm(tail) if first else tail, *state]
    in_specs = [SMEM, SMEM] + [VMEM] * (len(args) - 2)
    scratch = [pltpu.VMEM((rows + 2 * HB, columns, width), jnp.bfloat16)]
    if last:
        out_shape = [pltpu.HBM(held.shape, jnp.bfloat16)]
        out_specs = [ANY]
        scratch = [pltpu.VMEM(held.shape, jnp.bfloat16)] + scratch
    else:
        out_shape = [
            jax.ShapeDtypeStruct(held.shape, jnp.bfloat16),
            jax.ShapeDtypeStruct(held.shape, jnp.float32),
        ]
        out_shape += [edge] if count == 2 else [edge, edge]
        if first:
            in_specs[6] = ANY
            out_shape.append(jax.ShapeDtypeStruct(tail.shape, tail.dtype))
        out_specs = [VMEM] * len(out_shape)
    scratch.append(pltpu.SemaphoreType.DMA((rows // UNROLL,)))
    size = tail.size
    return pl.pallas_call(
        functools.partial(step_kernel, first, last, count),
        out_shape=out_shape,
        in_specs=in_specs,
        out_specs=out_specs,
        scratch_shapes=scratch,
        compiler_params=pltpu.CompilerParams(vmem_limit_bytes=8 * 2**20),
        cost_estimate=pl.CostEstimate(
            flops=2 * size * columns, bytes_accessed=2 * size, transcendentals=0
        ),
        name="filter_step",
    )(*args)


def join_kernel(*refs):
    out = refs[-1]
    for index in range(out.shape[0]):
        out[index : index + 1] = refs[index][...]


def join(pieces, after):
    return pl.pallas_call(
        join_kernel,
        out_shape=jax.ShapeDtypeStruct((len(pieces),) + pieces[0].shape[1:], jnp.bfloat16),
        in_specs=[VMEM] * len(pieces) + [ANY],
        out_specs=VMEM,
        compiler_params=pltpu.CompilerParams(vmem_limit_bytes=2 * 2**20),
        name="join",
    )(*pieces, after)


def exchange(count, edges):
    if count == 2:
        received = lax.ppermute(edges[0], "row", [(0, 1), (1, 0)])
        return received, received
    first, last = edges
    forward = [(i, i + 1) for i in range(count - 1)]
    backward = [(i + 1, i) for i in range(count - 1)]
    return lax.ppermute(last, "row", forward), lax.ppermute(first, "row", backward)


def meet(array, code):
    pairs = [(i, i ^ code) for i in range(lax.axis_size("vec"))]
    return lax.ppermute(array, "vec", pairs)


def assemble_kernel(low, place, *refs):
    parts = 1 << low
    shards = refs[: 2 * parts]
    out, ordered = refs[2 * parts :]
    vec, _, half, total = ordered.shape
    side, me = place[1], place[2]
    for index in range(2 * parts):
        owner, part = index // parts, index % parts
        for slot in range(vec // parts):
            ordered[me ^ (slot << low | part), side ^ owner] = shards[index][slot]
    columns = 2 * half
    span = max(1, 256 // columns)
    wide = span * columns
    unit = identity(wide)
    for start in range(0, vec, span):
        rows = ordered[start : start + span].reshape(wide, total)
        for left in range(0, total, wide):
            out[left : left + wide, start * columns : (start + span) * columns] = turned_by(
                unit, rows[:, left : left + wide]
            )


def assemble(place, mine, theirs):
    parts = len(mine)
    slots, half, total = mine[0].shape
    return pl.pallas_call(
        functools.partial(assemble_kernel, parts.bit_length() - 1),
        out_shape=jax.ShapeDtypeStruct((total, total), jnp.bfloat16),
        in_specs=[SMEM] + [VMEM] * (2 * parts),
        out_specs=VMEM,
        scratch_shapes=[pltpu.VMEM((parts * slots, 2, half, total), jnp.bfloat16)],
        compiler_params=pltpu.CompilerParams(vmem_limit_bytes=8 * 2**20),
        cost_estimate=pl.CostEstimate(
            flops=512 * total * total, bytes_accessed=4 * total * total, transcendentals=0
        ),
        name="assemble",
    )(place, *mine, *theirs)


def rotate_kernel(filtered, rotation, out, rows, leaving, sent):
    _, groups, _, width = filtered.shape
    total = rotation.shape[0]
    wide = leaving.shape[2]
    unit = identity(width)
    for group in range(groups):
        turned = filtered[:, group].reshape(total, width)
        for start in range(0, total, wide):
            rows[group * width : (group + 1) * width, start : start + wide] = turned_by(
                unit, turned[start : start + wide]
            )
    copies = []
    for chunk in range(total // wide):
        some = slice(chunk * wide, (chunk + 1) * wide)
        leaving[chunk] = jnp.dot(
            rows[...], rotation[:, some], preferred_element_type=jnp.float32
        ).astype(jnp.bfloat16)
        copies.append(pltpu.make_async_copy(leaving.at[chunk], out.at[:, some], sent.at[chunk]))
        copies[-1].start()
    for copy in copies:
        copy.wait()


def rotate(filtered, rotation):
    vec, groups, columns, width = filtered.shape
    rows, total = groups * width, vec * columns
    wide = min(256, total)
    return pl.pallas_call(
        rotate_kernel,
        out_shape=pltpu.HBM((rows, total), jnp.bfloat16),
        in_specs=[VMEM, VMEM],
        out_specs=ANY,
        scratch_shapes=[
            pltpu.VMEM((rows, total), jnp.bfloat16),
            pltpu.VMEM((total // wide, rows, wide), jnp.bfloat16),
            pltpu.SemaphoreType.DMA((total // wide,)),
        ],
        compiler_params=pltpu.CompilerParams(vmem_limit_bytes=16 * 2**20),
        name="rotate",
    )(filtered, rotation)


def local(vectors, rotation, blocks, column_blocks):
    vec, count = lax.axis_size("vec"), lax.axis_size("row")
    rows, total = vectors.shape[1:]
    columns = total // vec
    width = blocks.shape[-1]
    lanes = min(rows, width)
    groups = rows // lanes
    part = width // lanes
    row = lax.axis_index("row")
    place = jnp.stack([row, row & 1, lax.axis_index("vec")]).astype(jnp.int32)
    listing = jnp.transpose(column_blocks)
    bits = vec.bit_length() - 1
    low = max(0, bits - DIRECT)

    sent, half = prepare(place, vectors, jnp.transpose(rotation), groups, lanes)
    got = lax.all_to_all(sent, "vec", split_axis=0, concat_axis=0, tiled=True)
    pieces = [half]
    for code in range(1, vec >> low):
        pieces.append(meet(half, code << low))
    tail = turn_blocks(blocks, UNROLL, blocks.shape[0] - UNROLL)
    head = turn_blocks(blocks, 0, UNROLL)
    held = got.reshape(-1, part, columns, lanes).swapaxes(1, 2).reshape(-1, columns, width)

    if count == 2:
        start = jnp.where(row == 0, held.shape[0] - HB, 0)
        edges = [lax.dynamic_slice_in_dim(held, start, HB)]
    else:
        edges = [held[:HB], held[held.shape[0] - HB :]]
    operand, state = held, ()
    older, newer = None, held
    head = load_head(head)
    for turn in range(STEPS):
        halo = exchange(count, edges)
        outs = filter_step(turn, count, place, listing, operand, halo, head, tail, state)
        operand = outs[0]
        if turn == 0:
            outs, tail = outs[:-1], outs[-1]
            mine = [join(pieces, outs[2])]
        if turn < STEPS - 1:
            edges = outs[2 : 3 if count == 2 else 4]
            older, newer = newer, outs[1]
            state = (newer, older)
    for bit in range(low):
        more = []
        for array in mine:
            more.append(meet(array, 1 << bit))
        mine += more

    back = operand.reshape(-1, columns, part, lanes).swapaxes(1, 2)
    back = back.reshape(vec, groups, columns, lanes)
    returned = lax.all_to_all(back, "vec", split_axis=0, concat_axis=0, tiled=True)
    theirs = []
    for array in mine:
        theirs.append(lax.ppermute(array, "row", [(i, i ^ 1) for i in range(count)]))
    rotation = assemble(place, mine, theirs)
    return rotate(returned, rotation)[None]


def solution(mesh):
    placed = (P("row", "vec", None), P(None, "vec"), P("row", None, None, None), P("row", None))

    return jax.shard_map(
        local, mesh=mesh, in_specs=placed, out_specs=P("row", "vec", None), check_vma=False
    )
```

```python
import functools

import jax
import jax.numpy as jnp
from jax import lax
from jax.experimental import pallas as pl
from jax.experimental.pallas import tpu as pltpu
from jax.sharding import PartitionSpec as P


HB = 2
STEPS = 4
PARTS = 2
LOADS = 3
TURNED = 4
DIRECT = 2

centre = 0.3
half_width = 1.2

VMEM = pl.BlockSpec(memory_space=pltpu.VMEM)
SMEM = pl.BlockSpec(memory_space=pltpu.SMEM)
ANY = pl.BlockSpec(memory_space=pl.ANY)


def in_hbm(array):
    return pltpu.with_memory_space_constraint(array, pltpu.HBM)


def identity(size):
    rows = lax.broadcasted_iota(jnp.int32, (size, size), 0)
    columns = lax.broadcasted_iota(jnp.int32, (size, size), 1)
    return (rows == columns).astype(jnp.bfloat16)


def turned_by(unit, block):
    return lax.dot_general(
        unit, block, (((1,), (1,)), ((), ())), preferred_element_type=jnp.float32
    ).astype(jnp.bfloat16)


def prepare_kernel(place, vectors, shard, sent, half, landing, leaving, arrived, left, picked):
    chunks, span, groups, columns, lanes = leaving.shape
    wide = span * columns
    fetch = [
        pltpu.make_async_copy(
            vectors.at[0, pl.ds(group * lanes, lanes)],
            landing.at[pl.ds(group * lanes, lanes)],
            arrived.at[group],
        )
        for group in range(groups)
    ]
    pick = pltpu.make_async_copy(
        shard.at[pl.ds(pl.multiple_of(place[1] * half.shape[1], half.shape[1]), half.shape[1])],
        half.at[0],
        picked,
    )
    for copy in fetch:
        copy.start()
    pick.start()
    unit = identity(wide)
    for copy in fetch:
        copy.wait()
    copies = []
    for chunk in range(chunks):
        turned = turned_by(unit, landing[:, chunk * wide : (chunk + 1) * wide])
        for group in range(groups):
            leaving[chunk, :, group] = turned[:, group * lanes : (group + 1) * lanes].reshape(
                span, columns, lanes
            )
        copies.append(
            pltpu.make_async_copy(
                leaving.at[chunk], sent.at[pl.ds(chunk * span, span)], left.at[chunk]
            )
        )
        copies[-1].start()
    pick.wait()
    for copy in copies:
        copy.wait()


def prepare(place, vectors, shard, groups, lanes):
    columns, total = shard.shape
    wide = max(columns, min(256, total))
    chunks, span = total // wide, wide // columns
    return pl.pallas_call(
        prepare_kernel,
        out_shape=(
            pltpu.HBM((total // columns, groups, columns, lanes), jnp.bfloat16),
            jax.ShapeDtypeStruct((1, columns // 2, total), jnp.bfloat16),
        ),
        in_specs=[SMEM, ANY, ANY],
        out_specs=(ANY, VMEM),
        scratch_shapes=[
            pltpu.VMEM((groups * lanes, total), jnp.bfloat16),
            pltpu.VMEM((chunks, span, groups, columns, lanes), jnp.bfloat16),
            pltpu.SemaphoreType.DMA((groups,)),
            pltpu.SemaphoreType.DMA((chunks,)),
            pltpu.SemaphoreType.DMA,
        ],
        compiler_params=pltpu.CompilerParams(vmem_limit_bytes=8 * 2**20),
        name="prepare",
    )(place, in_hbm(vectors), in_hbm(shard))


def turn_kernel(blocks, turned):
    rows, listed, width = blocks.shape[:3]
    unit = identity(2 * width)
    for row in range(0, rows, 2):
        for j in range(0, listed, 2):
            square = jnp.concatenate(
                [
                    jnp.concatenate([blocks[row + k, j], blocks[row + k, j + 1]], axis=1)
                    for k in range(2)
                ],
                axis=0,
            )
            turned[row // 2, j * width : (j + 2) * width, :] = turned_by(unit, square)


def turn_blocks(blocks, first, rows, space):
    listed, width = blocks.shape[1:3]
    skipped = first // TURNED
    size = rows * listed * width * width
    return pl.pallas_call(
        turn_kernel,
        grid=(rows // TURNED,),
        out_shape=space((rows // 2, listed * width, 2 * width), jnp.bfloat16),
        in_specs=[
            pl.BlockSpec((TURNED, listed, width, width), lambda row: (row + skipped, 0, 0, 0))
        ],
        out_specs=pl.BlockSpec((TURNED // 2, listed * width, 2 * width), lambda row: (row, 0, 0)),
        compiler_params=pltpu.CompilerParams(vmem_limit_bytes=16 * 2**20),
        cost_estimate=pl.CostEstimate(
            flops=4 * width * size, bytes_accessed=4 * size, transcendentals=0
        ),
        name="turn_blocks",
    )(in_hbm(blocks))


def step_kernel(first, last, count, place, listing, held, low, high, *refs):
    parts, refs = list(refs[:PARTS]), list(refs[PARTS:])
    moved = refs.pop()
    field = refs.pop()
    listed, rows = listing.shape
    chunk = rows // 2 // 4
    if first:
        source, parts[-1] = parts[-1], refs.pop()

        piece = source.shape[0] // LOADS

        def load(index):
            some = pl.ds(index * piece, piece)
            return pltpu.make_async_copy(source.at[some], parts[-1].at[some], moved.at[index])

        for index in range(LOADS):
            load(index).start()
        previous = current = held
    else:
        current, previous = refs[:2]
        refs = refs[2:]
    if last:
        result, operand = refs

        def store(index):
            some = pl.ds(index * 2 * chunk, 2 * chunk)
            return pltpu.make_async_copy(operand.at[some], result.at[some], moved.at[index])

    else:
        operand = refs[0]
    columns, width = held.shape[1:]
    shift = place[0] * rows - HB
    field[HB : HB + rows] = held[...]
    if count == 2:
        received = low[...]
        nothing = jnp.zeros_like(received)
        field[:HB] = jnp.where(place[0] == 1, received, nothing)
        field[HB + rows :] = jnp.where(place[0] == 0, received, nothing)
    else:
        field[:HB] = low[...]
        field[HB + rows :] = high[...]

    def picked(row):
        return jnp.concatenate([field[listing[j, row] - shift] for j in range(listed)], axis=1)

    def finish(row, product):
        if first:
            following = (product - centre * current[row].astype(jnp.float32)) / half_width
        else:
            following = (
                2.0 * (product - centre * current[row]) / half_width
                - previous[row].astype(jnp.float32)
            )
        operand[row] = following.astype(jnp.bfloat16)
        if not last:
            refs[1][row] = following

    def multiply(part, begin, end, pair):
        for index in range(begin, end):
            both = jnp.concatenate([picked(2 * pair), picked(2 * pair + 1)], axis=0)
            product = jnp.dot(both, part[index], preferred_element_type=jnp.float32)
            finish(2 * pair, product[:columns, :width])
            finish(2 * pair + 1, product[columns:, width:])
            pair += 1
            if last and pair % chunk == 0:
                store(pair // chunk - 1).start()

    ready = parts[0].shape[0]
    if first:
        here = place[0] >= 0
        pl.when(here)(lambda: multiply(parts[0], 0, ready, 0))
        for index in range(LOADS):
            load(index).wait()
            begin = index * piece
            pl.when(here)(
                functools.partial(multiply, parts[1], begin, begin + piece, ready + begin)
            )
    else:
        multiply(parts[0], 0, ready, 0)
        multiply(parts[1], 0, parts[1].shape[0], ready)
    if last:
        for index in range(4):
            store(index).wait()
    elif count == 2:
        start = jnp.where(place[0] == 0, rows - HB, 0)
        refs[2][...] = operand[pl.ds(start, HB)]
    else:
        refs[2][...] = operand[:HB]
        refs[3][...] = operand[rows - HB :]


def filter_step(turn, count, place, listing, held, halo, parts, state):
    first, last = turn == 0, turn == STEPS - 1
    rows, columns, width = held.shape
    edge = jax.ShapeDtypeStruct((HB, columns, width), jnp.bfloat16)
    parts = list(parts)
    tail = parts[-1]
    if first:
        parts[-1] = in_hbm(tail)
    args = [place, listing, held, *halo, *parts, *state]
    in_specs = [SMEM, SMEM] + [VMEM] * (len(args) - 2)
    scratch = [pltpu.VMEM((rows + 2 * HB, columns, width), jnp.bfloat16)]
    if last:
        out_shape = [pltpu.HBM(held.shape, jnp.bfloat16)]
        out_specs = [ANY]
        scratch = [pltpu.VMEM(held.shape, jnp.bfloat16)] + scratch
    else:
        out_shape = [
            jax.ShapeDtypeStruct(held.shape, jnp.bfloat16),
            jax.ShapeDtypeStruct(held.shape, jnp.float32),
        ]
        out_shape += [edge] if count == 2 else [edge, edge]
        if first:
            in_specs[5 + PARTS - 1] = ANY
            out_shape.append(jax.ShapeDtypeStruct(tail.shape, tail.dtype))
        out_specs = [VMEM] * len(out_shape)
    scratch.append(pltpu.SemaphoreType.DMA((4,)))
    size = sum(part.size for part in parts)
    return pl.pallas_call(
        functools.partial(step_kernel, first, last, count),
        out_shape=out_shape,
        in_specs=in_specs,
        out_specs=out_specs,
        scratch_shapes=scratch,
        compiler_params=pltpu.CompilerParams(vmem_limit_bytes=8 * 2**20),
        cost_estimate=pl.CostEstimate(
            flops=2 * size * columns, bytes_accessed=2 * size, transcendentals=0
        ),
        name="filter_step",
    )(*args)


def join_kernel(*refs):
    out = refs[-1]
    for index in range(out.shape[0]):
        out[index : index + 1] = refs[index][...]


def join(pieces, after):
    return pl.pallas_call(
        join_kernel,
        out_shape=jax.ShapeDtypeStruct((len(pieces),) + pieces[0].shape[1:], jnp.bfloat16),
        in_specs=[VMEM] * len(pieces) + [ANY],
        out_specs=VMEM,
        compiler_params=pltpu.CompilerParams(vmem_limit_bytes=2 * 2**20),
        name="join",
    )(*pieces, after)


def exchange(count, edges):
    if count == 2:
        received = lax.ppermute(edges[0], "row", [(0, 1), (1, 0)])
        return received, received
    first, last = edges
    forward = [(i, i + 1) for i in range(count - 1)]
    backward = [(i + 1, i) for i in range(count - 1)]
    return lax.ppermute(last, "row", forward), lax.ppermute(first, "row", backward)


def meet(array, code):
    pairs = [(i, i ^ code) for i in range(lax.axis_size("vec"))]
    return lax.ppermute(array, "vec", pairs)


def assemble_kernel(low, place, *refs):
    parts = 1 << low
    shards = refs[: 2 * parts]
    out, ordered = refs[2 * parts :]
    vec, _, half, total = ordered.shape
    side, me = place[1], place[2]
    for index in range(2 * parts):
        owner, part = index // parts, index % parts
        for slot in range(vec // parts):
            ordered[me ^ (slot << low | part), side ^ owner] = shards[index][slot]
    columns = 2 * half
    span = max(1, 256 // columns)
    wide = span * columns
    unit = identity(wide)
    for start in range(0, vec, span):
        rows = ordered[start : start + span].reshape(wide, total)
        for left in range(0, total, wide):
            out[left : left + wide, start * columns : (start + span) * columns] = turned_by(
                unit, rows[:, left : left + wide]
            )


def assemble(place, mine, theirs):
    parts = len(mine)
    slots, half, total = mine[0].shape
    return pl.pallas_call(
        functools.partial(assemble_kernel, parts.bit_length() - 1),
        out_shape=jax.ShapeDtypeStruct((total, total), jnp.bfloat16),
        in_specs=[SMEM] + [VMEM] * (2 * parts),
        out_specs=VMEM,
        scratch_shapes=[pltpu.VMEM((parts * slots, 2, half, total), jnp.bfloat16)],
        compiler_params=pltpu.CompilerParams(vmem_limit_bytes=8 * 2**20),
        cost_estimate=pl.CostEstimate(
            flops=512 * total * total, bytes_accessed=4 * total * total, transcendentals=0
        ),
        name="assemble",
    )(place, *mine, *theirs)


def rotate_kernel(filtered, rotation, out, rows, leaving, sent):
    _, groups, _, width = filtered.shape
    total = rotation.shape[0]
    wide = leaving.shape[2]
    unit = identity(width)
    for group in range(groups):
        turned = filtered[:, group].reshape(total, width)
        for start in range(0, total, wide):
            rows[group * width : (group + 1) * width, start : start + wide] = turned_by(
                unit, turned[start : start + wide]
            )
    copies = []
    for chunk in range(total // wide):
        some = slice(chunk * wide, (chunk + 1) * wide)
        leaving[chunk] = jnp.dot(
            rows[...], rotation[:, some], preferred_element_type=jnp.float32
        ).astype(jnp.bfloat16)
        copies.append(pltpu.make_async_copy(leaving.at[chunk], out.at[:, some], sent.at[chunk]))
        copies[-1].start()
    for copy in copies:
        copy.wait()


def rotate(filtered, rotation):
    vec, groups, columns, width = filtered.shape
    rows, total = groups * width, vec * columns
    wide = min(256, total)
    return pl.pallas_call(
        rotate_kernel,
        out_shape=pltpu.HBM((rows, total), jnp.bfloat16),
        in_specs=[VMEM, VMEM],
        out_specs=ANY,
        scratch_shapes=[
            pltpu.VMEM((rows, total), jnp.bfloat16),
            pltpu.VMEM((total // wide, rows, wide), jnp.bfloat16),
            pltpu.SemaphoreType.DMA((total // wide,)),
        ],
        compiler_params=pltpu.CompilerParams(vmem_limit_bytes=16 * 2**20),
        name="rotate",
    )(filtered, rotation)


def local(vectors, rotation, blocks, column_blocks):
    vec, count = lax.axis_size("vec"), lax.axis_size("row")
    rows, total = vectors.shape[1:]
    columns = total // vec
    width = blocks.shape[-1]
    lanes = min(rows, width)
    groups = rows // lanes
    part = width // lanes
    row = lax.axis_index("row")
    place = jnp.stack([row, row & 1, lax.axis_index("vec")]).astype(jnp.int32)
    listing = jnp.transpose(column_blocks)
    bits = vec.bit_length() - 1
    low = max(0, bits - DIRECT)

    sent, half = prepare(place, vectors, jnp.transpose(rotation), groups, lanes)
    got = lax.all_to_all(sent, "vec", split_axis=0, concat_axis=0, tiled=True)
    pieces = [half]
    for code in range(1, vec >> low):
        if code == 3:
            pieces.append(meet(pieces[2], 1 << low))
        else:
            pieces.append(meet(half, code << low))
    quarter = blocks.shape[0] // 4
    tail = turn_blocks(blocks, quarter, 3 * quarter, pltpu.HBM)
    head = turn_blocks(blocks, 0, quarter, jax.ShapeDtypeStruct)
    held = got.reshape(-1, part, columns, lanes).swapaxes(1, 2).reshape(-1, columns, width)

    if count == 2:
        start = jnp.where(row == 0, held.shape[0] - HB, 0)
        edges = [lax.dynamic_slice_in_dim(held, start, HB)]
    else:
        edges = [held[:HB], held[held.shape[0] - HB :]]
    mine = [join(pieces, edges[0])]
    operand, state = held, ()
    older, newer = None, held
    parts = [head, tail]
    for turn in range(STEPS):
        halo = exchange(count, edges)
        outs = filter_step(turn, count, place, listing, operand, halo, parts, state)
        operand = outs[0]
        if turn == 0:
            outs, parts[-1] = outs[:-1], outs[-1]
        if turn < STEPS - 1:
            edges = outs[2 : 3 if count == 2 else 4]
            older, newer = newer, outs[1]
            state = (newer, older)
    for bit in range(low):
        more = []
        for array in mine:
            more.append(meet(array, 1 << bit))
        mine += more

    back = operand.reshape(-1, columns, part, lanes).swapaxes(1, 2)
    back = back.reshape(vec, groups, columns, lanes)
    returned = lax.all_to_all(back, "vec", split_axis=0, concat_axis=0, tiled=True)
    theirs = []
    for array in mine:
        theirs.append(lax.ppermute(array, "row", [(i, i ^ 1) for i in range(count)]))
    rotation = assemble(place, mine, theirs)
    return rotate(returned, rotation)[None]


def solution(mesh):
    placed = (P("row", "vec", None), P(None, "vec"), P("row", None, None, None), P("row", None))

    return jax.shard_map(
        local, mesh=mesh, in_specs=placed, out_specs=P("row", "vec", None), check_vma=False
    )
```

```python
import functools

import jax
import jax.numpy as jnp
from jax import lax
from jax.experimental import pallas as pl
from jax.experimental.pallas import tpu as pltpu
from jax.sharding import PartitionSpec as P


HB = 2
STEPS = 4
PARTS = 2
LOADS = 3
TURNED = 4
DIRECT = 2

centre = 0.3
half_width = 1.2

VMEM = pl.BlockSpec(memory_space=pltpu.VMEM)
SMEM = pl.BlockSpec(memory_space=pltpu.SMEM)
ANY = pl.BlockSpec(memory_space=pl.ANY)


def in_hbm(array):
    return pltpu.with_memory_space_constraint(array, pltpu.HBM)


def identity(size):
    rows = lax.broadcasted_iota(jnp.int32, (size, size), 0)
    columns = lax.broadcasted_iota(jnp.int32, (size, size), 1)
    return (rows == columns).astype(jnp.bfloat16)


def turned_by(unit, block):
    return lax.dot_general(
        unit, block, (((1,), (1,)), ((), ())), preferred_element_type=jnp.float32
    ).astype(jnp.bfloat16)


def prepare_kernel(place, vectors, shard, sent, half, landing, leaving, arrived, left, picked):
    chunks, span, groups, columns, lanes = leaving.shape
    wide = span * columns
    fetch = [
        pltpu.make_async_copy(
            vectors.at[0, pl.ds(group * lanes, lanes)],
            landing.at[pl.ds(group * lanes, lanes)],
            arrived.at[group],
        )
        for group in range(groups)
    ]
    pick = pltpu.make_async_copy(
        shard.at[pl.ds(pl.multiple_of(place[1] * half.shape[1], half.shape[1]), half.shape[1])],
        half.at[0],
        picked,
    )
    for copy in fetch:
        copy.start()
    pick.start()
    unit = identity(wide)
    for copy in fetch:
        copy.wait()
    copies = []
    for chunk in range(chunks):
        turned = turned_by(unit, landing[:, chunk * wide : (chunk + 1) * wide])
        for group in range(groups):
            leaving[chunk, :, group] = turned[:, group * lanes : (group + 1) * lanes].reshape(
                span, columns, lanes
            )
        copies.append(
            pltpu.make_async_copy(
                leaving.at[chunk], sent.at[pl.ds(chunk * span, span)], left.at[chunk]
            )
        )
        copies[-1].start()
    pick.wait()
    for copy in copies:
        copy.wait()


def prepare(place, vectors, shard, groups, lanes):
    columns, total = shard.shape
    wide = max(columns, min(256, total))
    chunks, span = total // wide, wide // columns
    return pl.pallas_call(
        prepare_kernel,
        out_shape=(
            pltpu.HBM((total // columns, groups, columns, lanes), jnp.bfloat16),
            jax.ShapeDtypeStruct((1, columns // 2, total), jnp.bfloat16),
        ),
        in_specs=[SMEM, ANY, ANY],
        out_specs=(ANY, VMEM),
        scratch_shapes=[
            pltpu.VMEM((groups * lanes, total), jnp.bfloat16),
            pltpu.VMEM((chunks, span, groups, columns, lanes), jnp.bfloat16),
            pltpu.SemaphoreType.DMA((groups,)),
            pltpu.SemaphoreType.DMA((chunks,)),
            pltpu.SemaphoreType.DMA,
        ],
        compiler_params=pltpu.CompilerParams(vmem_limit_bytes=8 * 2**20),
        name="prepare",
    )(place, in_hbm(vectors), in_hbm(shard))


def turn_kernel(blocks, turned):
    rows, listed, width = blocks.shape[:3]
    unit = identity(2 * width)
    for row in range(0, rows, 2):
        for j in range(0, listed, 2):
            square = jnp.concatenate(
                [
                    jnp.concatenate([blocks[row + k, j], blocks[row + k, j + 1]], axis=1)
                    for k in range(2)
                ],
                axis=0,
            )
            turned[row // 2, j * width : (j + 2) * width, :] = turned_by(unit, square)


def turn_blocks(blocks, first, rows, space):
    listed, width = blocks.shape[1:3]
    skipped = first // TURNED
    size = rows * listed * width * width
    return pl.pallas_call(
        turn_kernel,
        grid=(rows // TURNED,),
        out_shape=space((rows // 2, listed * width, 2 * width), jnp.bfloat16),
        in_specs=[
            pl.BlockSpec((TURNED, listed, width, width), lambda row: (row + skipped, 0, 0, 0))
        ],
        out_specs=pl.BlockSpec((TURNED // 2, listed * width, 2 * width), lambda row: (row, 0, 0)),
        compiler_params=pltpu.CompilerParams(vmem_limit_bytes=16 * 2**20),
        cost_estimate=pl.CostEstimate(
            flops=4 * width * size, bytes_accessed=4 * size, transcendentals=0
        ),
        name="turn_blocks",
    )(in_hbm(blocks))


def step_kernel(first, last, count, place, listing, held, low, high, *refs):
    parts, refs = list(refs[:PARTS]), list(refs[PARTS:])
    moved = refs.pop()
    listed, rows = listing.shape
    chunk = rows // 2 // 4
    operand = refs.pop() if last else None
    field = refs.pop()
    if first:
        source, parts[-1] = parts[-1], refs.pop()

        piece = source.shape[0] // LOADS

        def load(index):
            some = pl.ds(index * piece, piece)
            return pltpu.make_async_copy(source.at[some], parts[-1].at[some], moved.at[index])

        for index in range(LOADS):
            load(index).start()
        previous = current = held
    else:
        current, previous = refs[:2]
        refs = refs[2:]
    if last:
        (result,) = refs

        def store(index):
            some = pl.ds(index * 2 * chunk, 2 * chunk)
            return pltpu.make_async_copy(operand.at[some], result.at[some], moved.at[index])

    else:
        operand = refs[0]
    columns, width = held.shape[1:]
    shift = place[0] * rows - HB
    base = 0 if last else HB
    if first:
        field[HB : HB + rows] = held[...]
    if count == 2:
        received = low[...]
        nothing = jnp.zeros_like(received)
        field[:HB] = jnp.where(place[0] == 1, received, nothing)
        field[HB + rows :] = jnp.where(place[0] == 0, received, nothing)
    else:
        field[:HB] = low[...]
        field[HB + rows :] = high[...]

    def picked(row):
        return jnp.concatenate([field[listing[j, row] - shift] for j in range(listed)], axis=1)

    def finish(row, product):
        if first:
            following = (product - centre * current[row].astype(jnp.float32)) / half_width
        else:
            following = (
                2.0 * (product - centre * current[row]) / half_width
                - previous[row].astype(jnp.float32)
            )
        operand[base + row] = following.astype(jnp.bfloat16)
        if not last:
            refs[1][row] = following

    def multiply(part, begin, end, pair):
        for index in range(begin, end):
            both = jnp.concatenate([picked(2 * pair), picked(2 * pair + 1)], axis=0)
            product = jnp.dot(both, part[index], preferred_element_type=jnp.float32)
            finish(2 * pair, product[:columns, :width])
            finish(2 * pair + 1, product[columns:, width:])
            pair += 1
            if last and pair % chunk == 0:
                store(pair // chunk - 1).start()

    ready = parts[0].shape[0]
    if first:
        here = place[0] >= 0
        pl.when(here)(lambda: multiply(parts[0], 0, ready, 0))
        for index in range(LOADS):
            load(index).wait()
            begin = index * piece
            pl.when(here)(
                functools.partial(multiply, parts[1], begin, begin + piece, ready + begin)
            )
    else:
        multiply(parts[0], 0, ready, 0)
        multiply(parts[1], 0, parts[1].shape[0], ready)
    if last:
        for index in range(4):
            store(index).wait()
    elif count == 2:
        start = jnp.where(place[0] == 0, rows, HB)
        refs[2][...] = operand[pl.ds(start, HB)]
    else:
        refs[2][...] = operand[HB : 2 * HB]
        refs[3][...] = operand[rows : rows + HB]


def filter_step(turn, count, place, listing, held, halo, parts, state):
    first, last = turn == 0, turn == STEPS - 1
    columns, width = held.shape[1:]
    rows = listing.shape[1]
    edge = jax.ShapeDtypeStruct((HB, columns, width), jnp.bfloat16)
    parts = list(parts)
    tail = parts[-1]
    if first:
        parts[-1] = in_hbm(tail)
    args = [place, listing, held, *halo, *parts, *state]
    in_specs = [SMEM, SMEM] + [VMEM] * (len(args) - 2)
    field = jax.ShapeDtypeStruct((rows + 2 * HB, columns, width), jnp.bfloat16)
    scratch, aliases = [], {}
    if last:
        out_shape = [pltpu.HBM((rows, columns, width), jnp.bfloat16)]
        out_specs = [ANY]
        scratch = [pltpu.VMEM((rows, columns, width), jnp.bfloat16)]
    else:
        out_shape = [field, jax.ShapeDtypeStruct((rows, columns, width), jnp.float32)]
        out_shape += [edge] if count == 2 else [edge, edge]
        if first:
            in_specs[5 + PARTS - 1] = ANY
            out_shape.append(jax.ShapeDtypeStruct(tail.shape, tail.dtype))
            scratch = [pltpu.VMEM(field.shape, field.dtype)]
        out_specs = [VMEM] * len(out_shape)
    if not first:
        aliases = {2: len(out_shape)}
        out_shape.append(field)
        out_specs.append(VMEM)
    scratch.append(pltpu.SemaphoreType.DMA((4,)))
    size = sum(part.size for part in parts)
    return pl.pallas_call(
        functools.partial(step_kernel, first, last, count),
        out_shape=out_shape,
        in_specs=in_specs,
        out_specs=out_specs,
        input_output_aliases=aliases,
        scratch_shapes=scratch,
        compiler_params=pltpu.CompilerParams(vmem_limit_bytes=8 * 2**20),
        cost_estimate=pl.CostEstimate(
            flops=2 * size * columns, bytes_accessed=2 * size, transcendentals=0
        ),
        name="filter_step",
    )(*args)


def join_kernel(*refs):
    out = refs[-1]
    for index in range(out.shape[0]):
        out[index : index + 1] = refs[index][...]


def join(pieces, after):
    return pl.pallas_call(
        join_kernel,
        out_shape=jax.ShapeDtypeStruct((len(pieces),) + pieces[0].shape[1:], jnp.bfloat16),
        in_specs=[VMEM] * len(pieces) + [ANY],
        out_specs=VMEM,
        compiler_params=pltpu.CompilerParams(vmem_limit_bytes=2 * 2**20),
        name="join",
    )(*pieces, after)


def exchange(count, edges):
    if count == 2:
        received = lax.ppermute(edges[0], "row", [(0, 1), (1, 0)])
        return received, received
    first, last = edges
    forward = [(i, i + 1) for i in range(count - 1)]
    backward = [(i + 1, i) for i in range(count - 1)]
    return lax.ppermute(last, "row", forward), lax.ppermute(first, "row", backward)


def meet(array, code):
    pairs = [(i, i ^ code) for i in range(lax.axis_size("vec"))]
    return lax.ppermute(array, "vec", pairs)


def assemble_kernel(low, place, *refs):
    parts = 1 << low
    shards = refs[: 2 * parts]
    out, ordered = refs[2 * parts :]
    vec, _, half, total = ordered.shape
    side, me = place[1], place[2]
    for index in range(2 * parts):
        owner, part = index // parts, index % parts
        for slot in range(vec // parts):
            ordered[me ^ (slot << low | part), side ^ owner] = shards[index][slot]
    columns = 2 * half
    span = max(1, 256 // columns)
    wide = span * columns
    unit = identity(wide)
    for start in range(0, vec, span):
        rows = ordered[start : start + span].reshape(wide, total)
        for left in range(0, total, wide):
            out[left : left + wide, start * columns : (start + span) * columns] = turned_by(
                unit, rows[:, left : left + wide]
            )


def assemble(place, mine, theirs):
    parts = len(mine)
    slots, half, total = mine[0].shape
    return pl.pallas_call(
        functools.partial(assemble_kernel, parts.bit_length() - 1),
        out_shape=jax.ShapeDtypeStruct((total, total), jnp.bfloat16),
        in_specs=[SMEM] + [VMEM] * (2 * parts),
        out_specs=VMEM,
        scratch_shapes=[pltpu.VMEM((parts * slots, 2, half, total), jnp.bfloat16)],
        compiler_params=pltpu.CompilerParams(vmem_limit_bytes=8 * 2**20),
        cost_estimate=pl.CostEstimate(
            flops=512 * total * total, bytes_accessed=4 * total * total, transcendentals=0
        ),
        name="assemble",
    )(place, *mine, *theirs)


def rotate_kernel(filtered, rotation, out, rows, leaving, sent):
    _, groups, _, width = filtered.shape
    total = rotation.shape[0]
    wide = leaving.shape[2]
    unit = identity(width)
    for group in range(groups):
        turned = filtered[:, group].reshape(total, width)
        for start in range(0, total, wide):
            rows[group * width : (group + 1) * width, start : start + wide] = turned_by(
                unit, turned[start : start + wide]
            )
    copies = []
    for chunk in range(total // wide):
        some = slice(chunk * wide, (chunk + 1) * wide)
        leaving[chunk] = jnp.dot(
            rows[...], rotation[:, some], preferred_element_type=jnp.float32
        ).astype(jnp.bfloat16)
        copies.append(pltpu.make_async_copy(leaving.at[chunk], out.at[:, some], sent.at[chunk]))
        copies[-1].start()
    for copy in copies:
        copy.wait()


def rotate(filtered, rotation):
    vec, groups, columns, width = filtered.shape
    rows, total = groups * width, vec * columns
    wide = min(256, total)
    return pl.pallas_call(
        rotate_kernel,
        out_shape=pltpu.HBM((rows, total), jnp.bfloat16),
        in_specs=[VMEM, VMEM],
        out_specs=ANY,
        scratch_shapes=[
            pltpu.VMEM((rows, total), jnp.bfloat16),
            pltpu.VMEM((total // wide, rows, wide), jnp.bfloat16),
            pltpu.SemaphoreType.DMA((total // wide,)),
        ],
        compiler_params=pltpu.CompilerParams(vmem_limit_bytes=16 * 2**20),
        name="rotate",
    )(filtered, rotation)


def local(vectors, rotation, blocks, column_blocks):
    vec, count = lax.axis_size("vec"), lax.axis_size("row")
    rows, total = vectors.shape[1:]
    columns = total // vec
    width = blocks.shape[-1]
    lanes = min(rows, width)
    groups = rows // lanes
    part = width // lanes
    row = lax.axis_index("row")
    place = jnp.stack([row, row & 1, lax.axis_index("vec")]).astype(jnp.int32)
    listing = jnp.transpose(column_blocks)
    bits = vec.bit_length() - 1
    low = max(0, bits - DIRECT)

    sent, half = prepare(place, vectors, jnp.transpose(rotation), groups, lanes)
    got = lax.all_to_all(sent, "vec", split_axis=0, concat_axis=0, tiled=True)
    pieces = [half]
    for code in range(1, vec >> low):
        if code == 3:
            pieces.append(meet(pieces[2], 1 << low))
        else:
            pieces.append(meet(half, code << low))
    quarter = blocks.shape[0] // 4
    tail = turn_blocks(blocks, quarter, 3 * quarter, pltpu.HBM)
    head = turn_blocks(blocks, 0, quarter, jax.ShapeDtypeStruct)
    held = got.reshape(-1, part, columns, lanes).swapaxes(1, 2).reshape(-1, columns, width)

    if count == 2:
        start = jnp.where(row == 0, held.shape[0] - HB, 0)
        edges = [lax.dynamic_slice_in_dim(held, start, HB)]
    else:
        edges = [held[:HB], held[held.shape[0] - HB :]]
    mine = [join(pieces, edges[0])]
    operand, state = held, ()
    older, newer = None, held
    parts = [head, tail]
    for turn in range(STEPS):
        halo = exchange(count, edges)
        outs = filter_step(turn, count, place, listing, operand, halo, parts, state)
        operand = outs[0]
        if turn == 0:
            outs, parts[-1] = outs[:-1], outs[-1]
        if turn < STEPS - 1:
            edges = outs[2 : 3 if count == 2 else 4]
            older, newer = newer, outs[1]
            state = (newer, older)
    for bit in range(low):
        more = []
        for array in mine:
            more.append(meet(array, 1 << bit))
        mine += more

    back = operand.reshape(-1, columns, part, lanes).swapaxes(1, 2)
    back = back.reshape(vec, groups, columns, lanes)
    returned = lax.all_to_all(back, "vec", split_axis=0, concat_axis=0, tiled=True)
    theirs = []
    for array in mine:
        theirs.append(lax.ppermute(array, "row", [(i, i ^ 1) for i in range(count)]))
    rotation = assemble(place, mine, theirs)
    return rotate(returned, rotation)[None]


def solution(mesh):
    placed = (P("row", "vec", None), P(None, "vec"), P("row", None, None, None), P("row", None))

    return jax.shard_map(
        local, mesh=mesh, in_specs=placed, out_specs=P("row", "vec", None), check_vma=False
    )
```

```python
import functools

import jax
import jax.numpy as jnp
from jax import lax
from jax.experimental import pallas as pl
from jax.experimental.pallas import tpu as pltpu
from jax.sharding import PartitionSpec as P


HB = 2
STEPS = 4
PARTS = 2
LOADS = 6
TURNED = 8
DIRECT = 2

centre = 0.3
half_width = 1.2

VMEM = pl.BlockSpec(memory_space=pltpu.VMEM)
SMEM = pl.BlockSpec(memory_space=pltpu.SMEM)
ANY = pl.BlockSpec(memory_space=pl.ANY)


def in_hbm(array):
    return pltpu.with_memory_space_constraint(array, pltpu.HBM)


def identity(size):
    rows = lax.broadcasted_iota(jnp.int32, (size, size), 0)
    columns = lax.broadcasted_iota(jnp.int32, (size, size), 1)
    return (rows == columns).astype(jnp.bfloat16)


def turned_by(unit, block):
    return lax.dot_general(
        unit, block, (((1,), (1,)), ((), ())), preferred_element_type=jnp.float32
    ).astype(jnp.bfloat16)


def prepare_kernel(place, vectors, shard, sent, half, landing, leaving, arrived, left, picked):
    chunks, span, groups, columns, lanes = leaving.shape
    wide = span * columns
    fetch = [
        pltpu.make_async_copy(
            vectors.at[0, pl.ds(group * lanes, lanes)],
            landing.at[pl.ds(group * lanes, lanes)],
            arrived.at[group],
        )
        for group in range(groups)
    ]
    pick = pltpu.make_async_copy(
        shard.at[pl.ds(pl.multiple_of(place[1] * half.shape[1], half.shape[1]), half.shape[1])],
        half.at[0],
        picked,
    )
    for copy in fetch:
        copy.start()
    pick.start()
    unit = identity(wide)
    for copy in fetch:
        copy.wait()
    copies = []
    for chunk in range(chunks):
        turned = turned_by(unit, landing[:, chunk * wide : (chunk + 1) * wide])
        for group in range(groups):
            leaving[chunk, :, group] = turned[:, group * lanes : (group + 1) * lanes].reshape(
                span, columns, lanes
            )
        copies.append(
            pltpu.make_async_copy(
                leaving.at[chunk], sent.at[pl.ds(chunk * span, span)], left.at[chunk]
            )
        )
        copies[-1].start()
    pick.wait()
    for copy in copies:
        copy.wait()


def prepare(place, vectors, shard, groups, lanes):
    columns, total = shard.shape
    wide = max(columns, min(256, total))
    chunks, span = total // wide, wide // columns
    return pl.pallas_call(
        prepare_kernel,
        out_shape=(
            pltpu.HBM((total // columns, groups, columns, lanes), jnp.bfloat16),
            jax.ShapeDtypeStruct((1, columns // 2, total), jnp.bfloat16),
        ),
        in_specs=[SMEM, ANY, ANY],
        out_specs=(ANY, VMEM),
        scratch_shapes=[
            pltpu.VMEM((groups * lanes, total), jnp.bfloat16),
            pltpu.VMEM((chunks, span, groups, columns, lanes), jnp.bfloat16),
            pltpu.SemaphoreType.DMA((groups,)),
            pltpu.SemaphoreType.DMA((chunks,)),
            pltpu.SemaphoreType.DMA,
        ],
        compiler_params=pltpu.CompilerParams(vmem_limit_bytes=8 * 2**20),
        name="prepare",
    )(place, in_hbm(vectors), in_hbm(shard))


def turn_kernel(blocks, turned):
    rows, listed, width = blocks.shape[:3]
    unit = identity(2 * width)
    for row in range(0, rows, 2):
        for j in range(0, listed, 2):
            square = jnp.concatenate(
                [
                    jnp.concatenate([blocks[row + k, j], blocks[row + k, j + 1]], axis=1)
                    for k in range(2)
                ],
                axis=0,
            )
            turned[row // 2, j * width : (j + 2) * width, :] = turned_by(unit, square)


def turn_blocks(blocks, first, rows, space):
    listed, width = blocks.shape[1:3]
    skipped = first // TURNED
    size = rows * listed * width * width
    return pl.pallas_call(
        turn_kernel,
        grid=(rows // TURNED,),
        out_shape=space((rows // 2, listed * width, 2 * width), jnp.bfloat16),
        in_specs=[
            pl.BlockSpec((TURNED, listed, width, width), lambda row: (row + skipped, 0, 0, 0))
        ],
        out_specs=pl.BlockSpec((TURNED // 2, listed * width, 2 * width), lambda row: (row, 0, 0)),
        compiler_params=pltpu.CompilerParams(vmem_limit_bytes=16 * 2**20),
        cost_estimate=pl.CostEstimate(
            flops=4 * width * size, bytes_accessed=4 * size, transcendentals=0
        ),
        name="turn_blocks",
    )(in_hbm(blocks))


def step_kernel(first, last, count, place, listing, held, low, high, *refs):
    parts, refs = list(refs[:PARTS]), list(refs[PARTS:])
    moved = refs.pop()
    listed, rows = listing.shape
    chunk = rows // 2 // 4
    operand = refs.pop() if last else None
    field = refs.pop()
    if first:
        source, parts[-1] = parts[-1], refs.pop()

        piece = source.shape[0] // LOADS

        def load(index):
            some = pl.ds(index * piece, piece)
            return pltpu.make_async_copy(source.at[some], parts[-1].at[some], moved.at[index])

        for index in range(LOADS):
            load(index).start()
        previous = current = held
    else:
        current, previous = refs[:2]
        refs = refs[2:]
    if last:
        (result,) = refs

        def store(index):
            some = pl.ds(index * 2 * chunk, 2 * chunk)
            return pltpu.make_async_copy(operand.at[some], result.at[some], moved.at[index])

    else:
        operand = refs[0]
    columns, width = held.shape[1:]
    shift = place[0] * rows - HB
    base = 0 if last else HB
    if first:
        field[HB : HB + rows] = held[...]
    if count == 2:
        received = low[...]
        nothing = jnp.zeros_like(received)
        field[:HB] = jnp.where(place[0] == 1, received, nothing)
        field[HB + rows :] = jnp.where(place[0] == 0, received, nothing)
    else:
        field[:HB] = low[...]
        field[HB + rows :] = high[...]

    def picked(row):
        return jnp.concatenate([field[listing[j, row] - shift] for j in range(listed)], axis=1)

    def finish(row, product):
        if first:
            following = (product - centre * current[row].astype(jnp.float32)) / half_width
        else:
            following = (
                2.0 * (product - centre * current[row]) / half_width
                - previous[row].astype(jnp.float32)
            )
        operand[base + row] = following.astype(jnp.bfloat16)
        if not last:
            refs[1][row] = following

    def multiply(part, begin, end, pair):
        for index in range(begin, end):
            both = jnp.concatenate([picked(2 * pair), picked(2 * pair + 1)], axis=0)
            product = jnp.dot(both, part[index], preferred_element_type=jnp.float32)
            finish(2 * pair, product[:columns, :width])
            finish(2 * pair + 1, product[columns:, width:])
            pair += 1
            if last and pair % chunk == 0:
                store(pair // chunk - 1).start()

    ready = parts[0].shape[0]
    if first:
        here = place[0] >= 0
        pl.when(here)(lambda: multiply(parts[0], 0, ready, 0))
        for index in range(LOADS):
            load(index).wait()
            begin = index * piece
            pl.when(here)(
                functools.partial(multiply, parts[1], begin, begin + piece, ready + begin)
            )
    else:
        multiply(parts[0], 0, ready, 0)
        multiply(parts[1], 0, parts[1].shape[0], ready)
    if last:
        for index in range(4):
            store(index).wait()
    elif count == 2:
        start = jnp.where(place[0] == 0, rows, HB)
        refs[2][...] = operand[pl.ds(start, HB)]
    else:
        refs[2][...] = operand[HB : 2 * HB]
        refs[3][...] = operand[rows : rows + HB]


def filter_step(turn, count, place, listing, held, halo, parts, state):
    first, last = turn == 0, turn == STEPS - 1
    columns, width = held.shape[1:]
    rows = listing.shape[1]
    edge = jax.ShapeDtypeStruct((HB, columns, width), jnp.bfloat16)
    parts = list(parts)
    tail = parts[-1]
    if first:
        parts[-1] = in_hbm(tail)
    args = [place, listing, held, *halo, *parts, *state]
    in_specs = [SMEM, SMEM] + [VMEM] * (len(args) - 2)
    field = jax.ShapeDtypeStruct((rows + 2 * HB, columns, width), jnp.bfloat16)
    scratch, aliases = [], {}
    if last:
        out_shape = [pltpu.HBM((rows, columns, width), jnp.bfloat16)]
        out_specs = [ANY]
        scratch = [pltpu.VMEM((rows, columns, width), jnp.bfloat16)]
    else:
        out_shape = [field, jax.ShapeDtypeStruct((rows, columns, width), jnp.float32)]
        out_shape += [edge] if count == 2 else [edge, edge]
        if first:
            in_specs[5 + PARTS - 1] = ANY
            out_shape.append(jax.ShapeDtypeStruct(tail.shape, tail.dtype))
            scratch = [pltpu.VMEM(field.shape, field.dtype)]
        out_specs = [VMEM] * len(out_shape)
    if not first:
        aliases = {2: len(out_shape)}
        out_shape.append(field)
        out_specs.append(VMEM)
    scratch.append(pltpu.SemaphoreType.DMA((8,)))
    size = sum(part.size for part in parts)
    return pl.pallas_call(
        functools.partial(step_kernel, first, last, count),
        out_shape=out_shape,
        in_specs=in_specs,
        out_specs=out_specs,
        input_output_aliases=aliases,
        scratch_shapes=scratch,
        compiler_params=pltpu.CompilerParams(vmem_limit_bytes=8 * 2**20),
        cost_estimate=pl.CostEstimate(
            flops=2 * size * columns, bytes_accessed=2 * size, transcendentals=0
        ),
        name="filter_step",
    )(*args)


def join_kernel(*refs):
    out = refs[-1]
    for index in range(out.shape[0]):
        out[index : index + 1] = refs[index][...]


def join(pieces, after):
    return pl.pallas_call(
        join_kernel,
        out_shape=jax.ShapeDtypeStruct((len(pieces),) + pieces[0].shape[1:], jnp.bfloat16),
        in_specs=[VMEM] * len(pieces) + [ANY],
        out_specs=VMEM,
        compiler_params=pltpu.CompilerParams(vmem_limit_bytes=2 * 2**20),
        name="join",
    )(*pieces, after)


def exchange(count, edges):
    if count == 2:
        received = lax.ppermute(edges[0], "row", [(0, 1), (1, 0)])
        return received, received
    first, last = edges
    forward = [(i, i + 1) for i in range(count - 1)]
    backward = [(i + 1, i) for i in range(count - 1)]
    return lax.ppermute(last, "row", forward), lax.ppermute(first, "row", backward)


def meet(array, code):
    pairs = [(i, i ^ code) for i in range(lax.axis_size("vec"))]
    return lax.ppermute(array, "vec", pairs)


def assemble_kernel(low, place, *refs):
    parts = 1 << low
    shards = refs[: 2 * parts]
    out, ordered = refs[2 * parts :]
    vec, _, half, total = ordered.shape
    side, me = place[1], place[2]
    for index in range(2 * parts):
        owner, part = index // parts, index % parts
        for slot in range(vec // parts):
            ordered[me ^ (slot << low | part), side ^ owner] = shards[index][slot]
    columns = 2 * half
    span = max(1, 256 // columns)
    wide = span * columns
    unit = identity(wide)
    for start in range(0, vec, span):
        rows = ordered[start : start + span].reshape(wide, total)
        for left in range(0, total, wide):
            out[left : left + wide, start * columns : (start + span) * columns] = turned_by(
                unit, rows[:, left : left + wide]
            )


def assemble(place, mine, theirs):
    parts = len(mine)
    slots, half, total = mine[0].shape
    return pl.pallas_call(
        functools.partial(assemble_kernel, parts.bit_length() - 1),
        out_shape=jax.ShapeDtypeStruct((total, total), jnp.bfloat16),
        in_specs=[SMEM] + [VMEM] * (2 * parts),
        out_specs=VMEM,
        scratch_shapes=[pltpu.VMEM((parts * slots, 2, half, total), jnp.bfloat16)],
        compiler_params=pltpu.CompilerParams(vmem_limit_bytes=8 * 2**20),
        cost_estimate=pl.CostEstimate(
            flops=512 * total * total, bytes_accessed=4 * total * total, transcendentals=0
        ),
        name="assemble",
    )(place, *mine, *theirs)


def rotate_kernel(filtered, rotation, out, rows, leaving, sent):
    _, groups, _, width = filtered.shape
    total = rotation.shape[0]
    wide = leaving.shape[2]
    unit = identity(width)
    for group in range(groups):
        turned = filtered[:, group].reshape(total, width)
        for start in range(0, total, wide):
            rows[group * width : (group + 1) * width, start : start + wide] = turned_by(
                unit, turned[start : start + wide]
            )
    copies = []
    for chunk in range(total // wide):
        some = slice(chunk * wide, (chunk + 1) * wide)
        leaving[chunk] = jnp.dot(
            rows[...], rotation[:, some], preferred_element_type=jnp.float32
        ).astype(jnp.bfloat16)
        copies.append(pltpu.make_async_copy(leaving.at[chunk], out.at[:, some], sent.at[chunk]))
        copies[-1].start()
    for copy in copies:
        copy.wait()


def rotate(filtered, rotation):
    vec, groups, columns, width = filtered.shape
    rows, total = groups * width, vec * columns
    wide = min(256, total)
    return pl.pallas_call(
        rotate_kernel,
        out_shape=pltpu.HBM((rows, total), jnp.bfloat16),
        in_specs=[VMEM, VMEM],
        out_specs=ANY,
        scratch_shapes=[
            pltpu.VMEM((rows, total), jnp.bfloat16),
            pltpu.VMEM((total // wide, rows, wide), jnp.bfloat16),
            pltpu.SemaphoreType.DMA((total // wide,)),
        ],
        compiler_params=pltpu.CompilerParams(vmem_limit_bytes=16 * 2**20),
        name="rotate",
    )(filtered, rotation)


def local(vectors, rotation, blocks, column_blocks):
    vec, count = lax.axis_size("vec"), lax.axis_size("row")
    rows, total = vectors.shape[1:]
    columns = total // vec
    width = blocks.shape[-1]
    lanes = min(rows, width)
    groups = rows // lanes
    part = width // lanes
    row = lax.axis_index("row")
    place = jnp.stack([row, row & 1, lax.axis_index("vec")]).astype(jnp.int32)
    listing = jnp.transpose(column_blocks)
    bits = vec.bit_length() - 1
    low = max(0, bits - DIRECT)

    sent, half = prepare(place, vectors, jnp.transpose(rotation), groups, lanes)
    got = lax.all_to_all(sent, "vec", split_axis=0, concat_axis=0, tiled=True)
    pieces = [half]
    for code in range(1, vec >> low):
        if code == 3:
            pieces.append(meet(pieces[2], 1 << low))
        else:
            pieces.append(meet(half, code << low))
    quarter = blocks.shape[0] // 4
    tail = turn_blocks(blocks, quarter, 3 * quarter, pltpu.HBM)
    head = turn_blocks(blocks, 0, quarter, jax.ShapeDtypeStruct)
    held = got.reshape(-1, part, columns, lanes).swapaxes(1, 2).reshape(-1, columns, width)

    if count == 2:
        start = jnp.where(row == 0, held.shape[0] - HB, 0)
        edges = [lax.dynamic_slice_in_dim(held, start, HB)]
    else:
        edges = [held[:HB], held[held.shape[0] - HB :]]
    mine = [join(pieces, edges[0])]
    operand, state = held, ()
    older, newer = None, held
    parts = [head, tail]
    for turn in range(STEPS):
        halo = exchange(count, edges)
        outs = filter_step(turn, count, place, listing, operand, halo, parts, state)
        operand = outs[0]
        if turn == 0:
            outs, parts[-1] = outs[:-1], outs[-1]
        if turn < STEPS - 1:
            edges = outs[2 : 3 if count == 2 else 4]
            older, newer = newer, outs[1]
            state = (newer, older)
    for bit in range(low):
        more = []
        for array in mine:
            more.append(meet(array, 1 << bit))
        mine += more

    back = operand.reshape(-1, columns, part, lanes).swapaxes(1, 2)
    back = back.reshape(vec, groups, columns, lanes)
    returned = lax.all_to_all(back, "vec", split_axis=0, concat_axis=0, tiled=True)
    theirs = []
    for array in mine:
        theirs.append(lax.ppermute(array, "row", [(i, i ^ 1) for i in range(count)]))
    rotation = assemble(place, mine, theirs)
    return rotate(returned, rotation)[None]


def solution(mesh):
    placed = (P("row", "vec", None), P(None, "vec"), P("row", None, None, None), P("row", None))

    return jax.shard_map(
        local, mesh=mesh, in_specs=placed, out_specs=P("row", "vec", None), check_vma=False
    )
```
